32 devices in a mesh: sub: 8 (over z, y), blk: 4 (over x, core).
Axes of the slice: x: 2, y: 2, z: 4, core: 2. Of those that a mesh axis runs over, the one named last changes fastest.
Arguments:
- initial_state: float32 [8, 64, 2048], P('sub', None, 'blk'), may hold values from -6 to 6
- source: bfloat16 [8, 8, 64, 2048], P('sub', None, None, 'blk'), may hold values from -6 to 6
- inverse_diag: float32 [8, 2048], P('sub', 'blk'), may hold values from 0.5 to 0.85
- inverse_off: bfloat16 [8, 2048, 2048], P('sub', None, 'blk'), may hold values from -0.032958984 to 0.032958984
- coupling: float32 [8, 128], P('sub', 'blk'), may hold values from 0.3 to 3
- initial_waves: bfloat16 [8, 128, 512], P('sub', 'blk'), may hold values from -6 to 6
- bucket: int32 [8], P('sub'), may hold values from 0 to 2
- partner: int32 [8, 128], P('sub', 'blk'), may hold values from 0 to 7
- position_of: int32 [8], replicated, may hold values from 0 to 7, each once
Outputs:
- last_state: float32 [8, 64, 2048], P('sub', None, 'blk')
- waveform: float32 [8, 128, 512], P('sub', 'blk')
The draws below stay inside these ranges and needn't reach their ends.
Inputs may be any that keep to these rules, and one draw needn't show every extreme that they name: A subcircuit of bucket b takes 8 / 2 ** (2 - b) implicit Euler steps. `position_of`: a permutation.
All inputs are finite; a program needn't handle non-finite values.
Results may differ from the reference program's by a relative error of at most 0.0052.
Values may be sent and summed in bfloat16 or wider, within the bound.
A program may use at most 64 MiB of HBM per device.

```python
import math
import jax
import jax.numpy as jnp
from jax import lax

NODES = 2048
PORTS = 128
STEPS = 8
SWEEPS = 2
INPUT_CASES = 64
SUBS = 8


def place_ends(values, rng, low, high):
    index_at = [jax.random.randint(jax.random.fold_in(rng, axis), (), 0, length) for axis, length in enumerate(values.shape)]
    longest = values.shape.index(max(values.shape))
    neighbour = index_at[:longest] + [(index_at[longest] + 1) % values.shape[longest]] + index_at[longest + 1:]
    return values.at[tuple(index_at)].set(low).at[tuple(neighbour)].set(high)


def block_levels(stream_key, shape, pieces, smallest, high):
    loudness, own = 1.0, jax.random.fold_in(stream_key, 6)
    for axis_at, shards_of in pieces:
        draws = jnp.exp(jax.random.uniform(jax.random.fold_in(own, axis_at), (shards_of,), jnp.float32, smallest / len(pieces), high / len(pieces)))
        loudness = loudness * jnp.repeat(draws, shape[axis_at] // shards_of).reshape([-1 if axis == axis_at else 1 for axis in range(len(shape))])
    return loudness


def gaussian(rng, shape, width, limit, cuts=(), kind=jnp.bfloat16):
    drawn = jax.random.normal(rng, shape, jnp.float32) * width
    if len(cuts) > 0:
        drawn = block_levels(rng, shape, cuts, -0.22, 0.18) * drawn
    return jnp.clip(drawn, min=-limit, max=limit).astype(kind)


def setup_inputs(seed: int = 0) -> dict:
    streams_of = jax.random.split(jax.random.key(seed), 10)
    initial_state = gaussian(streams_of[0], (SUBS, INPUT_CASES, NODES), 1.0, 6.0, ((0, 8), (2, 4)), jnp.float32)
    source = gaussian(streams_of[1], (SUBS, STEPS, INPUT_CASES, NODES), 0.5, 6.0, ((0, 8), (3, 4)))
    inverse_diag = jnp.clip(0.5 + 0.35000002 * jax.random.uniform(streams_of[2], (SUBS, NODES), jnp.float32) ** block_levels(streams_of[2], (SUBS, NODES), ((0, 8), (1, 4)), -0.2, 0.2), 0.5, 0.85)
    inverse_off = gaussian(streams_of[3], (SUBS, NODES, NODES), (0.25 * NODES ** -0.5), 0.032958984, ((0, 8), (2, 4)))
    coupling = jnp.clip(jnp.exp(math.log(3.0) - 2.3025851 * jax.random.uniform(streams_of[4], (SUBS, PORTS), jnp.float32) ** block_levels(streams_of[4], (SUBS, PORTS), ((0, 8), (1, 4)), -0.2, 0.2)), 0.3, 3.0)
    initial_waves = gaussian(streams_of[5], (SUBS, PORTS, STEPS * INPUT_CASES), 1.0, 6.0, ((0, 8), (1, 4)))
    bucket = place_ends(jax.random.randint(streams_of[6], (SUBS,), 0, 3), jax.random.fold_in(streams_of[6], 1), 0, 2).astype(jnp.int32)
    partner = place_ends(jax.random.randint(streams_of[7], (SUBS, PORTS), 0, SUBS), jax.random.fold_in(streams_of[7], 1), 0, SUBS - 1).astype(jnp.int32)
    position_of = jax.random.permutation(streams_of[8], SUBS).astype(jnp.int32)
    return dict(initial_state=initial_state, source=source, inverse_diag=inverse_diag, inverse_off=inverse_off, coupling=coupling, initial_waves=initial_waves, bucket=bucket, partner=partner, position_of=position_of)


def step_count(bucket):
    return jnp.where(bucket == 0, STEPS // 4, jnp.where(bucket == 1, STEPS // 2, STEPS)).astype(jnp.int32)


def evolve(initial_state, source, inverse_diag, inverse_off, coupling, bucket, incoming):
    corners = initial_state.shape[0]
    stride = NODES // PORTS
    step_total = step_count(bucket)
    spacing = (STEPS // step_total).astype(jnp.int32)
    spacing_float = spacing.astype(jnp.float32)
    driven = incoming.astype(jnp.float32).reshape(PORTS, STEPS, corners)

    def advance(time_step_index, carried):
        current, sample_times = carried
        fine_index = ((time_step_index + 1) * spacing - 1).astype(jnp.int32)
        forcing = lax.dynamic_index_in_dim(source, fine_index, 0, keepdims=False).astype(jnp.float32)
        injected = coupling[:, None] * lax.dynamic_index_in_dim(driven, fine_index, 1, keepdims=False)
        spread = jnp.pad(injected.T[:, :, None], ((0, 0), (0, 0), (0, stride - 1))).reshape(corners, NODES)
        loop_argument = (current + spacing_float * (forcing + spread)).astype(jnp.bfloat16)
        loop_argument = lax.optimization_barrier(loop_argument)
        updated = inverse_diag[None, :] * loop_argument.astype(jnp.float32) + jnp.dot(loop_argument, inverse_off, preferred_element_type=jnp.float32)
        port_values = updated.reshape(corners, PORTS, stride)[:, :, 0]
        sample_times = lax.dynamic_update_index_in_dim(sample_times, port_values, time_step_index, 0)
        return updated, sample_times

    sample_times = jnp.zeros((STEPS, corners, PORTS), jnp.float32)
    last_state, sample_times = lax.fori_loop(0, step_total, advance, (initial_state, sample_times))
    held_index = jnp.arange(STEPS, dtype=jnp.int32) // spacing
    waveform = jnp.transpose(sample_times[held_index], (2, 0, 1)).reshape(PORTS, STEPS * corners)
    return last_state, waveform


def reference(initial_state, source, inverse_diag, inverse_off, coupling, initial_waves, bucket, partner, position_of):
    located = position_of[partner]
    port_index = jnp.arange(PORTS, dtype=jnp.int32)[None, :]
    waves = initial_waves
    for sweep_index in range(SWEEPS):
        incoming = waves[located, port_index]
        last_state, waveform = lax.map(lambda members: evolve(*members), (initial_state, source, inverse_diag, inverse_off, coupling, bucket, incoming))
        waves = waveform.astype(jnp.bfloat16)
    return last_state, waveform
```

```python
import functools

import jax
import jax.numpy as jnp
from jax import lax
from jax.experimental import pallas as pl
from jax.experimental.pallas import tpu as pltpu
from jax.sharding import PartitionSpec as P

MESH = pl.DeviceIdType.MESH
BF16 = jnp.bfloat16
F32 = jnp.float32


def mm(a, b):
    return jnp.dot(a, b, preferred_element_type=F32)


def mm_nt(a, b):
    return lax.dot_general(a, b, (((1,), (1,)), ((), ())), preferred_element_type=F32)


def split(v):
    hi = v.astype(BF16)
    return hi, (v - hi.astype(F32)).astype(BF16)


def kernel(
    ns, nb,
    x0, src, dia, moff, cpl, w0, bkt, par, pos,
    last, wav,
    mats, buf, oper, z, hs, p_hi, p_lo, t_hi, t_lo, zp, inc8, rb, samp, wall, iall, call, lhs,
    m_sem, x_send, x_recv, w_send, w_recv, i_send, i_recv,
):
    me_s, me = lax.axis_index("sub"), lax.axis_index("blk")
    steps, rows, width = src.shape[1:]
    ports = cpl.shape[1]
    stride = width // ports
    all_ports = ports * nb
    halves = all_ports // rows
    near = me + 1 - 2 * lax.rem(me, 2)
    across = lax.rem(me + 2, nb)
    roles = (me, near, across, nb - 1 - me)

    loads = [
        pltpu.make_async_copy(
            moff.at[0, pl.ds(pl.multiple_of(b * width, width), width)], mats.at[r], m_sem.at[r]
        )
        for r, b in enumerate(roles)
    ]
    for load in loads:
        load.start()

    barrier = pltpu.get_barrier_semaphore()

    @pl.loop(1, ns)
    def _(d):
        pl.semaphore_signal(
            barrier, inc=1, device_id={"sub": lax.rem(me_s + d, ns)}, device_id_type=MESH
        )

    for peer in roles[1:]:
        pl.semaphore_signal(barrier, inc=1, device_id={"blk": peer}, device_id_type=MESH)

    bucket = bkt[0]
    count = jnp.where(bucket == 0, steps // 4, jnp.where(bucket == 1, steps // 2, steps))
    spacing = jnp.where(bucket == 0, 4, jnp.where(bucket == 1, 2, 1))
    spacing_f = spacing.astype(F32)

    def fine(j):
        return jnp.minimum((j + 1) * spacing - 1, steps - 1)

    def held(g):
        return jnp.where(bucket == 0, g // 4, jnp.where(bucket == 1, g // 2, g))

    def exchange(g, k, role):
        start, end, peer = {1: (0, 1, near), 2: (0, 2, across), 3: (2, 3, near)}[role]
        parity = lax.rem(k, 2)
        return pltpu.make_async_remote_copy(
            src_ref=buf.at[g, k, start],
            dst_ref=buf.at[g, k, end],
            send_sem=x_send.at[g, parity, role - 1],
            recv_sem=x_recv.at[g, parity, role - 1],
            device_id={"blk": peer},
            device_id_type=MESH,
        )

    def post(g, k, value):
        buf[g, k, 0] = value.astype(BF16)
        exchange(g, k, 2).start()
        exchange(g, k, 1).start()

    def finish(g, k):
        exchange(g, k, 2).wait_recv()
        exchange(g, k, 3).start()
        total = diagonal * oper[g] + mm(buf[g, k, 0], mats[0])
        exchange(g, k, 1).wait_recv()
        total += mm(buf[g, k, 1], mats[1])
        total += mm(buf[g, k, 2], mats[2])
        exchange(g, k, 3).wait_recv()
        total += mm(buf[g, k, 3], mats[3])
        for role in (1, 2, 3):
            exchange(g, k, role).wait_send()
        return total

    def wave_copy(t, d):
        return pltpu.make_async_remote_copy(
            src_ref=wall.at[t, me_s],
            dst_ref=wall.at[t, me_s],
            send_sem=w_send.at[t, d],
            recv_sem=w_recv.at[t, me_s],
            device_id={"sub": lax.rem(me_s + d, ns)},
            device_id_type=MESH,
        )

    def send_waves(t):
        @pl.loop(1, ns)
        def _(d):
            wave_copy(t, d).start()

    def wait_waves(t):
        @pl.loop(1, ns)
        def _(d):
            origin = lax.rem(me_s + d, ns)
            pltpu.make_async_remote_copy(
                src_ref=wall.at[t, origin],
                dst_ref=wall.at[t, origin],
                send_sem=w_send.at[t, d],
                recv_sem=w_recv.at[t, origin],
                device_id={"sub": origin},
                device_id_type=MESH,
            ).wait_recv()

    def block_copy(ref, t, r, owner):
        return pltpu.make_async_remote_copy(
            src_ref=ref.at[owner],
            dst_ref=ref.at[owner],
            send_sem=i_send.at[t, r],
            recv_sem=i_recv.at[t, owner],
            device_id={"blk": roles[r]},
            device_id_type=MESH,
        )

    def share(ref, t):
        for r in (2, 3, 1):
            block_copy(ref, t, r, me).start()

    def wait_share(ref, t):
        for r in (1, 2, 3):
            block_copy(ref, t, r, roles[r]).wait_recv()

    square = (
        lax.broadcasted_iota(jnp.int32, (ports, ports), 0)
        == lax.broadcasted_iota(jnp.int32, (ports, ports), 1)
    )

    def column(row):
        spread = jnp.broadcast_to(row, (ports, ports))
        return jnp.sum(jnp.where(square, spread, jnp.zeros_like(spread)), axis=1, keepdims=True)

    def select(t):
        owner = column(par[...].astype(F32))

        def place(i, found):
            return jnp.where(owner == i.astype(F32), pos[i].astype(F32), found)

        located = lax.fori_loop(0, ns, place, jnp.zeros((ports, 1), F32))

        def pick(q, chosen):
            return jnp.where(located == q.astype(F32), wall[t, q].astype(F32), chosen)

        chosen = lax.fori_loop(0, ns, pick, jnp.zeros(w0.shape[1:], F32))
        iall[t, me] = chosen.astype(BF16)

    def inputs(t):
        for b in range(nb):
            value = iall[t, b]
            for f in range(steps):
                inc8[f, b * ports : (b + 1) * ports, :] = value[:, f * rows : (f + 1) * rows]
        for j in range(steps):
            factor = jnp.where(j < count, spacing_f, 0.0)
            rb[j] = (inc8[fine(j)].astype(F32) * factor).astype(BF16)

    def respond():
        drive = rb[...].reshape(steps * all_ports, rows)
        value = mm(t_hi[...], drive) + mm(t_lo[...], drive)
        samp[...] = zp[...] + value.reshape(steps, ports, rows)

    diagonal = dia[...]
    pick_ports = (
        lax.broadcasted_iota(jnp.int32, (ports, width), 1)
        == stride * lax.broadcasted_iota(jnp.int32, (ports, width), 0)
    ).astype(F32).astype(BF16)

    z[...] = x0[0]
    wall[0, me_s] = w0[0]
    call[me] = jnp.broadcast_to(column(cpl[...]), call.shape[1:])
    first = x0[0] + spacing_f * src[0, fine(0)].astype(F32)
    oper[0] = first

    pl.semaphore_wait(barrier, ns - 1 + nb - 1)
    post(0, 0, first)
    share(call, 2)
    send_waves(0)
    t_hi[...] = jnp.zeros_like(t_hi)
    t_lo[...] = jnp.zeros_like(t_lo)
    for load in loads:
        load.wait()

    def keep(h, k, value):
        scale = call[...].reshape(all_ports, call.shape[2])[h * rows : (h + 1) * rows, :1]
        hi, lo = split(scale * value)
        hs[k, h * rows : (h + 1) * rows, :] = hi
        p_hi[k, :, h * rows : (h + 1) * rows] = mm_nt(pick_ports, hi).astype(BF16)
        p_lo[k, :, h * rows : (h + 1) * rows] = mm_nt(pick_ports, lo).astype(BF16)

    for h in range(halves):
        node = stride * (lax.broadcasted_iota(jnp.int32, (rows, width), 0) + h * rows)
        lane = lax.broadcasted_iota(jnp.int32, (rows, width), 1)
        total = diagonal * (lane + me * width == node).astype(F32)
        for r, b in enumerate(roles):
            total += mm((lane + b * width == node).astype(F32).astype(BF16), mats[r])
        oper[1 + h] = total
        post(1 + h, 1, total)
    wait_share(call, 2)
    for h in range(halves):
        keep(h, 0, oper[1 + h])

    @pl.loop(0, steps)
    def _(i):
        total = jnp.where(i < count, finish(0, i), z[...])
        z[...] = total

        @pl.when(i < steps - 1)
        def _():
            operand = total + spacing_f * src[0, fine(i + 1)].astype(F32)
            oper[0] = operand
            post(0, i + 1, operand)

        hi, lo = split(total)
        zp[i] = mm_nt(pick_ports, hi) + mm_nt(pick_ports, lo)

        @pl.when(i >= 1)
        def _():
            for h in range(halves):
                value = finish(1 + h, i)
                oper[1 + h] = value

                @pl.when(i < steps - 1)
                def _():
                    post(1 + h, i + 1, value)

                keep(h, i, value)

        @pl.when(i == steps // 2 - 1)
        def _():
            wait_waves(0)
            select(0)
            share(iall.at[0], 0)

        @pl.when(i == steps // 2 + 1)
        def _():
            wait_share(iall.at[0], 0)
            inputs(0)

    for k in range(steps):
        for j in range(k + 1):
            there = (
                slice(k * ports, (k + 1) * ports),
                slice(j * all_ports, (j + 1) * all_ports),
            )
            t_hi[there] = p_hi[k - j]
            t_lo[there] = p_lo[k - j]
    respond()
    for g in range(steps):
        wall[1, me_s, :, g * rows : (g + 1) * rows] = samp[held(g)].astype(BF16)
    send_waves(1)
    wait_waves(1)
    select(1)
    share(iall.at[1], 1)
    wait_share(iall.at[1], 1)
    inputs(1)
    respond()
    for g in range(steps):
        wav[0, :, g * rows : (g + 1) * rows] = samp[held(g)]
    unit = (
        lax.broadcasted_iota(jnp.int32, (rows, rows), 0)
        == lax.broadcasted_iota(jnp.int32, (rows, rows), 1)
    ).astype(F32).astype(BF16)
    for m in range(1, steps + 1):
        turned = mm_nt(unit, rb[jnp.maximum(count - m, 0)])
        lhs[:, (m - 1) * all_ports : m * all_ports] = jnp.where(m <= count, turned, 0.0).astype(BF16)
    last[0] = z[...] + mm(lhs[...], hs[...].reshape(steps * all_ports, width))

    for t in range(2):

        @pl.loop(1, ns)
        def _(d):
            wave_copy(t, d).wait_send()

        for r in (1, 2, 3):
            block_copy(iall.at[t], t, r, me).wait_send()
    for r in (1, 2, 3):
        block_copy(call, 2, r, me).wait_send()


def shards(ns, nb, initial_state, source, inverse_diag, inverse_off, coupling, initial_waves,
           bucket, partner, position_of):
    _, steps, rows, width = source.shape
    ports = coupling.shape[1]
    all_ports = ports * nb
    groups = 1 + all_ports // rows
    vmem = pl.BlockSpec(memory_space=pltpu.VMEM)
    smem = pl.BlockSpec(memory_space=pltpu.SMEM)
    dma = pltpu.SemaphoreType.DMA
    return pl.pallas_call(
        functools.partial(kernel, ns, nb),
        out_shape=(
            jax.ShapeDtypeStruct(initial_state.shape, F32),
            jax.ShapeDtypeStruct(initial_waves.shape, F32),
        ),
        in_specs=[vmem, vmem, vmem, pl.BlockSpec(memory_space=pl.ANY), vmem, vmem, smem, vmem, smem],
        out_specs=(vmem, vmem),
        scratch_shapes=[
            pltpu.VMEM((nb, width, width), BF16),
            pltpu.VMEM((groups, steps, nb, rows, width), BF16),
            pltpu.VMEM((groups, rows, width), F32),
            pltpu.VMEM((rows, width), F32),
            pltpu.VMEM((steps, all_ports, width), BF16),
            pltpu.VMEM((steps, ports, all_ports), BF16),
            pltpu.VMEM((steps, ports, all_ports), BF16),
            pltpu.VMEM((steps * ports, steps * all_ports), BF16),
            pltpu.VMEM((steps * ports, steps * all_ports), BF16),
            pltpu.VMEM((steps, ports, rows), F32),
            pltpu.VMEM((steps, all_ports, rows), BF16),
            pltpu.VMEM((steps, all_ports, rows), BF16),
            pltpu.VMEM((steps, ports, rows), F32),
            pltpu.VMEM((2, ns) + initial_waves.shape[1:], BF16),
            pltpu.VMEM((2, nb) + initial_waves.shape[1:], BF16),
            pltpu.VMEM((nb, ports, 128), F32),
            pltpu.VMEM((rows, steps * all_ports), BF16),
            dma((nb,)),
            dma((groups, 2, 3)),
            dma((groups, 2, 3)),
            dma((2, ns)),
            dma((2, ns)),
            dma((3, nb)),
            dma((3, nb)),
        ],
        compiler_params=pltpu.CompilerParams(
            collective_id=0, has_side_effects=True, vmem_limit_bytes=48 * 1024 * 1024
        ),
    )(initial_state, source, inverse_diag, inverse_off, coupling, initial_waves, bucket, partner,
      position_of)


def solution(mesh):
    return jax.shard_map(
        functools.partial(shards, mesh.shape["sub"], mesh.shape["blk"]),
        mesh=mesh,
        in_specs=(
            P("sub", None, "blk"),
            P("sub", None, None, "blk"),
            P("sub", "blk"),
            P("sub", None, "blk"),
            P("sub", "blk"),
            P("sub", "blk", None),
            P("sub"),
            P("sub", "blk"),
            P(),
        ),
        out_specs=(P("sub", None, "blk"), P("sub", "blk", None)),
        check_vma=False,
    )
```

```python
import functools

import jax
import jax.numpy as jnp
from jax import lax
from jax.experimental import pallas as pl
from jax.experimental.pallas import tpu as pltpu
from jax.sharding import PartitionSpec as P

MESH = pl.DeviceIdType.MESH
BF16 = jnp.bfloat16
F32 = jnp.float32


def mm(a, b):
    return jnp.dot(a, b, preferred_element_type=F32)


def mm_nt(a, b):
    return lax.dot_general(a, b, (((1,), (1,)), ((), ())), preferred_element_type=F32)


def split(v):
    hi = v.astype(BF16)
    return hi, (v - hi.astype(F32)).astype(BF16)


def kernel(
    ns, nb,
    x0_in, src_in, dia_in, moff, cpl_in, w0_in, bkt_in, par_in, pos_in,
    last, wav,
    src, dia, cpl, par, bkt, pos, mats, buf, oper, z, hs, p_hi, p_lo, t_hi, t_lo, zp, inc8, rb, samp, wall, iall, call, lhs,
    a_sem, m_sem, x_send, x_recv, w_send, w_recv, i_send, i_recv,
):
    me_s, me = lax.axis_index("sub"), lax.axis_index("blk")
    steps, rows, width = src.shape
    ports = cpl.shape[1]
    stride = width // ports
    all_ports = ports * nb
    halves = all_ports // rows
    near = me + 1 - 2 * lax.rem(me, 2)
    across = lax.rem(me + 2, nb)
    roles = (me, near, across, nb - 1 - me)

    args = [
        pltpu.make_async_copy(there, here, a_sem.at[r])
        for r, (there, here) in enumerate(
            (
                (bkt_in, bkt),
                (x0_in.at[0], z),
                (src_in.at[0], src),
                (cpl_in, cpl),
                (w0_in.at[0], wall.at[0, me_s]),
                (dia_in, dia),
                (par_in, par),
                (pos_in, pos),
            )
        )
    ]
    for load in args:
        load.start()
    loads = [
        pltpu.make_async_copy(
            moff.at[0, pl.ds(pl.multiple_of(b * width, width), width)], mats.at[r], m_sem.at[r]
        )
        for r, b in enumerate(roles)
    ]
    for load in loads:
        load.start()

    barrier = pltpu.get_barrier_semaphore()

    @pl.loop(1, ns)
    def _(d):
        pl.semaphore_signal(
            barrier, inc=1, device_id={"sub": lax.rem(me_s + d, ns)}, device_id_type=MESH
        )

    for peer in roles[1:]:
        pl.semaphore_signal(barrier, inc=1, device_id={"blk": peer}, device_id_type=MESH)

    for load in args:
        load.wait()
    bucket = bkt[0]
    count = jnp.where(bucket == 0, steps // 4, jnp.where(bucket == 1, steps // 2, steps))
    spacing = jnp.where(bucket == 0, 4, jnp.where(bucket == 1, 2, 1))
    spacing_f = spacing.astype(F32)

    def fine(j):
        return jnp.minimum((j + 1) * spacing - 1, steps - 1)

    def held(g):
        return jnp.where(bucket == 0, g // 4, jnp.where(bucket == 1, g // 2, g))

    def exchange(g, k, role):
        start, end, peer = {1: (0, 1, near), 2: (0, 2, across), 3: (2, 3, near)}[role]
        parity = lax.rem(k, 2)
        return pltpu.make_async_remote_copy(
            src_ref=buf.at[g, k, start],
            dst_ref=buf.at[g, k, end],
            send_sem=x_send.at[g, parity, role - 1],
            recv_sem=x_recv.at[g, parity, role - 1],
            device_id={"blk": peer},
            device_id_type=MESH,
        )

    def post(g, k, value):
        buf[g, k, 0] = value.astype(BF16)
        exchange(g, k, 2).start()
        exchange(g, k, 1).start()

    def finish(g, k, meanwhile):
        exchange(g, k, 2).wait_recv()
        exchange(g, k, 3).start()
        meanwhile()
        total = diagonal * oper[g] + mm(buf[g, k, 0], mats[0])
        exchange(g, k, 1).wait_recv()
        total += mm(buf[g, k, 1], mats[1])
        total += mm(buf[g, k, 2], mats[2])
        exchange(g, k, 3).wait_recv()
        total += mm(buf[g, k, 3], mats[3])
        for role in (1, 2, 3):
            exchange(g, k, role).wait_send()
        return total

    def wave_copy(t, d):
        return pltpu.make_async_remote_copy(
            src_ref=wall.at[t, me_s],
            dst_ref=wall.at[t, me_s],
            send_sem=w_send.at[t, d],
            recv_sem=w_recv.at[t, me_s],
            device_id={"sub": lax.rem(me_s + d, ns)},
            device_id_type=MESH,
        )

    def send_waves(t):
        @pl.loop(1, ns)
        def _(d):
            wave_copy(t, d).start()

    def wait_waves(t):
        @pl.loop(1, ns)
        def _(d):
            origin = lax.rem(me_s + d, ns)
            pltpu.make_async_remote_copy(
                src_ref=wall.at[t, origin],
                dst_ref=wall.at[t, origin],
                send_sem=w_send.at[t, d],
                recv_sem=w_recv.at[t, origin],
                device_id={"sub": origin},
                device_id_type=MESH,
            ).wait_recv()

    def block_copy(ref, t, r, owner):
        return pltpu.make_async_remote_copy(
            src_ref=ref.at[owner],
            dst_ref=ref.at[owner],
            send_sem=i_send.at[t, r],
            recv_sem=i_recv.at[t, owner],
            device_id={"blk": roles[r]},
            device_id_type=MESH,
        )

    def share(ref, t):
        for r in (2, 3, 1):
            block_copy(ref, t, r, me).start()

    def wait_share(ref, t):
        for r in (1, 2, 3):
            block_copy(ref, t, r, roles[r]).wait_recv()

    square = (
        lax.broadcasted_iota(jnp.int32, (ports, ports), 0)
        == lax.broadcasted_iota(jnp.int32, (ports, ports), 1)
    )

    def column(row):
        spread = jnp.broadcast_to(row, (ports, ports))
        return jnp.sum(jnp.where(square, spread, jnp.zeros_like(spread)), axis=1, keepdims=True)

    def select(t):
        owner = column(par[...].astype(F32))

        def place(i, found):
            return jnp.where(owner == i.astype(F32), pos[i].astype(F32), found)

        located = lax.fori_loop(0, ns, place, jnp.zeros((ports, 1), F32))

        def pick(q, chosen):
            return jnp.where(located == q.astype(F32), wall[t, q].astype(F32), chosen)

        chosen = lax.fori_loop(0, ns, pick, jnp.zeros(wall.shape[2:], F32))
        iall[t, me] = chosen.astype(BF16)

    def inputs(t):
        for b in range(nb):
            value = iall[t, b]
            for f in range(steps):
                inc8[f, b * ports : (b + 1) * ports, :] = value[:, f * rows : (f + 1) * rows]
        for j in range(steps):
            factor = jnp.where(j < count, spacing_f, 0.0)
            rb[j] = (inc8[fine(j)].astype(F32) * factor).astype(BF16)

    def respond():
        drive = rb[...].reshape(steps * all_ports, rows)
        value = mm(t_hi[...], drive) + mm(t_lo[...], drive)
        samp[...] = zp[...] + value.reshape(steps, ports, rows)

    diagonal = dia[...]
    pick_ports = (
        lax.broadcasted_iota(jnp.int32, (ports, width), 1)
        == stride * lax.broadcasted_iota(jnp.int32, (ports, width), 0)
    ).astype(F32).astype(BF16)

    call[me] = jnp.broadcast_to(column(cpl[...]), call.shape[1:])
    first = z[...] + spacing_f * src[fine(0)].astype(F32)
    oper[0] = first

    pl.semaphore_wait(barrier, ns - 1 + nb - 1)
    post(0, 0, first)
    share(call, 2)
    send_waves(0)
    t_hi[...] = jnp.zeros_like(t_hi)
    t_lo[...] = jnp.zeros_like(t_lo)
    for load in loads:
        load.wait()

    def keep(h, k):
        value = oper[1 + h]
        scale = call[...].reshape(all_ports, call.shape[2])[h * rows : (h + 1) * rows, :1]
        hi, lo = split(scale * value)
        hs[k, h * rows : (h + 1) * rows, :] = hi
        p_hi[k, :, h * rows : (h + 1) * rows] = mm_nt(pick_ports, hi).astype(BF16)
        p_lo[k, :, h * rows : (h + 1) * rows] = mm_nt(pick_ports, lo).astype(BF16)

    for h in range(halves):
        node = stride * (lax.broadcasted_iota(jnp.int32, (rows, width), 0) + h * rows)
        lane = lax.broadcasted_iota(jnp.int32, (rows, width), 1)
        total = diagonal * (lane + me * width == node).astype(F32)
        for r, b in enumerate(roles):
            total += mm((lane + b * width == node).astype(F32).astype(BF16), mats[r])
        oper[1 + h] = total
        post(1 + h, 1, total)
    def sample(k):
        hi, lo = split(z[...])
        zp[k] = mm_nt(pick_ports, hi) + mm_nt(pick_ports, lo)

    def keep_last(k):
        @pl.when(k >= 0)
        def _():
            keep(halves - 1, k)

    wait_share(call, 2)
    for h in range(halves - 1):
        keep(h, 0)

    @pl.loop(0, steps)
    def _(i):
        total = jnp.where(i < count, finish(0, i, lambda: keep_last(i - 1)), z[...])
        z[...] = total

        @pl.when(i < steps - 1)
        def _():
            operand = total + spacing_f * src[fine(i + 1)].astype(F32)
            oper[0] = operand
            post(0, i + 1, operand)

        @pl.when(i == 0)
        def _():
            sample(0)

        @pl.when(i >= 1)
        def _():
            for h in range(halves):
                work = functools.partial(keep, h - 1, i) if h else functools.partial(sample, i)
                value = finish(1 + h, i, work)
                oper[1 + h] = value

                @pl.when(i < steps - 1)
                def _():
                    post(1 + h, i + 1, value)

        @pl.when(i == steps // 2 - 1)
        def _():
            wait_waves(0)
            select(0)
            share(iall.at[0], 0)

        @pl.when(i == steps // 2 + 1)
        def _():
            wait_share(iall.at[0], 0)
            inputs(0)

    keep(halves - 1, steps - 1)
    for k in range(steps):
        for j in range(k + 1):
            there = (
                slice(k * ports, (k + 1) * ports),
                slice(j * all_ports, (j + 1) * all_ports),
            )
            t_hi[there] = p_hi[k - j]
            t_lo[there] = p_lo[k - j]
    respond()
    for g in range(steps):
        wall[1, me_s, :, g * rows : (g + 1) * rows] = samp[held(g)].astype(BF16)
    send_waves(1)
    wait_waves(1)
    select(1)
    share(iall.at[1], 1)
    wait_share(iall.at[1], 1)
    inputs(1)
    respond()
    for g in range(steps):
        wav[0, :, g * rows : (g + 1) * rows] = samp[held(g)]
    unit = (
        lax.broadcasted_iota(jnp.int32, (rows, rows), 0)
        == lax.broadcasted_iota(jnp.int32, (rows, rows), 1)
    ).astype(F32).astype(BF16)
    for m in range(1, steps + 1):
        turned = mm_nt(unit, rb[jnp.maximum(count - m, 0)])
        lhs[:, (m - 1) * all_ports : m * all_ports] = jnp.where(m <= count, turned, 0.0).astype(BF16)
    last[0] = z[...] + mm(lhs[...], hs[...].reshape(steps * all_ports, width))

    for t in range(2):

        @pl.loop(1, ns)
        def _(d):
            wave_copy(t, d).wait_send()

        for r in (1, 2, 3):
            block_copy(iall.at[t], t, r, me).wait_send()
    for r in (1, 2, 3):
        block_copy(call, 2, r, me).wait_send()


def shards(ns, nb, initial_state, source, inverse_diag, inverse_off, coupling, initial_waves,
           bucket, partner, position_of):
    _, steps, rows, width = source.shape
    ports = coupling.shape[1]
    all_ports = ports * nb
    groups = 1 + all_ports // rows
    vmem = pl.BlockSpec(memory_space=pltpu.VMEM)
    dma = pltpu.SemaphoreType.DMA
    return pl.pallas_call(
        functools.partial(kernel, ns, nb),
        out_shape=(
            jax.ShapeDtypeStruct(initial_state.shape, F32),
            jax.ShapeDtypeStruct(initial_waves.shape, F32),
        ),
        in_specs=[pl.BlockSpec(memory_space=pl.ANY)] * 9,
        out_specs=(vmem, vmem),
        scratch_shapes=[
            pltpu.VMEM(source.shape[1:], BF16),
            pltpu.VMEM(inverse_diag.shape, F32),
            pltpu.VMEM(coupling.shape, F32),
            pltpu.VMEM(partner.shape, jnp.int32),
            pltpu.SMEM(bucket.shape, jnp.int32),
            pltpu.SMEM(position_of.shape, jnp.int32),
            pltpu.VMEM((nb, width, width), BF16),
            pltpu.VMEM((groups, steps, nb, rows, width), BF16),
            pltpu.VMEM((groups, rows, width), F32),
            pltpu.VMEM((rows, width), F32),
            pltpu.VMEM((steps, all_ports, width), BF16),
            pltpu.VMEM((steps, ports, all_ports), BF16),
            pltpu.VMEM((steps, ports, all_ports), BF16),
            pltpu.VMEM((steps * ports, steps * all_ports), BF16),
            pltpu.VMEM((steps * ports, steps * all_ports), BF16),
            pltpu.VMEM((steps, ports, rows), F32),
            pltpu.VMEM((steps, all_ports, rows), BF16),
            pltpu.VMEM((steps, all_ports, rows), BF16),
            pltpu.VMEM((steps, ports, rows), F32),
            pltpu.VMEM((2, ns) + initial_waves.shape[1:], BF16),
            pltpu.VMEM((2, nb) + initial_waves.shape[1:], BF16),
            pltpu.VMEM((nb, ports, 128), F32),
            pltpu.VMEM((rows, steps * all_ports), BF16),
            dma((8,)),
            dma((nb,)),
            dma((groups, 2, 3)),
            dma((groups, 2, 3)),
            dma((2, ns)),
            dma((2, ns)),
            dma((3, nb)),
            dma((3, nb)),
        ],
        compiler_params=pltpu.CompilerParams(
            collective_id=0, has_side_effects=True, vmem_limit_bytes=48 * 1024 * 1024
        ),
    )(initial_state, source, inverse_diag, inverse_off, coupling, initial_waves, bucket, partner,
      position_of)


def solution(mesh):
    return jax.shard_map(
        functools.partial(shards, mesh.shape["sub"], mesh.shape["blk"]),
        mesh=mesh,
        in_specs=(
            P("sub", None, "blk"),
            P("sub", None, None, "blk"),
            P("sub", "blk"),
            P("sub", None, "blk"),
            P("sub", "blk"),
            P("sub", "blk", None),
            P("sub"),
            P("sub", "blk"),
            P(),
        ),
        out_specs=(P("sub", None, "blk"), P("sub", "blk", None)),
        check_vma=False,
    )
```

```python
import functools

import jax
import jax.numpy as jnp
from jax import lax
from jax.experimental import pallas as pl
from jax.experimental.pallas import tpu as pltpu
from jax.sharding import PartitionSpec as P

MESH = pl.DeviceIdType.MESH
BF16 = jnp.bfloat16
F32 = jnp.float32


def mm(a, b):
    return jnp.dot(a, b, preferred_element_type=F32)


def mm_nt(a, b):
    return lax.dot_general(a, b, (((1,), (1,)), ((), ())), preferred_element_type=F32)


def split(v):
    hi = v.astype(BF16)
    return hi, (v - hi.astype(F32)).astype(BF16)


def kernel(
    ns, nb,
    x0_in, src_in, dia_in, moff, cpl_in, w0_in, bkt_in, par_in, pos_in,
    last, wav,
    src, dia, cpl, par, bkt, pos, mats, buf, oper, z, hs, p_hi, p_lo, t_hi, t_lo, zp, inc8, rb, samp, wall, iall, call, lhs,
    a_sem, m_sem, x_send, x_recv, w_send, w_recv, i_send, i_recv,
):
    me_s, me = lax.axis_index("sub"), lax.axis_index("blk")
    steps, rows, width = src.shape
    ports = cpl.shape[1]
    stride = width // ports
    all_ports = ports * nb
    halves = all_ports // rows
    near = me + 1 - 2 * lax.rem(me, 2)
    across = lax.rem(me + 2, nb)
    roles = (me, near, across, nb - 1 - me)

    args = [
        pltpu.make_async_copy(there, here, a_sem.at[r])
        for r, (there, here) in enumerate(
            (
                (bkt_in, bkt),
                (x0_in.at[0], z),
                (src_in.at[0], src),
                (cpl_in, cpl),
                (w0_in.at[0], wall.at[0, me_s]),
                (dia_in, dia),
                (par_in, par),
                (pos_in, pos),
            )
        )
    ]
    for load in args:
        load.start()
    loads = [
        pltpu.make_async_copy(
            moff.at[0, pl.ds(pl.multiple_of(b * width, width), width)], mats.at[r], m_sem.at[r]
        )
        for r, b in enumerate(roles)
    ]
    for load in loads:
        load.start()

    barrier = pltpu.get_barrier_semaphore()

    @pl.loop(1, ns)
    def _(d):
        pl.semaphore_signal(
            barrier, inc=1, device_id={"sub": lax.rem(me_s + d, ns)}, device_id_type=MESH
        )

    for peer in roles[1:]:
        pl.semaphore_signal(barrier, inc=1, device_id={"blk": peer}, device_id_type=MESH)

    for load in args:
        load.wait()
    bucket = bkt[0]
    count = jnp.where(bucket == 0, steps // 4, jnp.where(bucket == 1, steps // 2, steps))
    spacing = jnp.where(bucket == 0, 4, jnp.where(bucket == 1, 2, 1))
    spacing_f = spacing.astype(F32)

    def fine(j):
        return jnp.minimum((j + 1) * spacing - 1, steps - 1)

    def held(g):
        return jnp.where(bucket == 0, g // 4, jnp.where(bucket == 1, g // 2, g))

    def exchange(g, k, role):
        start, end, peer = {1: (0, 1, near), 2: (0, 2, across), 3: (2, 3, near)}[role]
        parity = lax.rem(k, 2)
        return pltpu.make_async_remote_copy(
            src_ref=buf.at[g, k, start],
            dst_ref=buf.at[g, k, end],
            send_sem=x_send.at[g, parity, role - 1],
            recv_sem=x_recv.at[g, parity, role - 1],
            device_id={"blk": peer},
            device_id_type=MESH,
        )

    def post(g, k, value):
        buf[g, k, 0] = value.astype(BF16)
        exchange(g, k, 2).start()
        exchange(g, k, 1).start()

    def finish(g, k, meanwhile):
        exchange(g, k, 2).wait_recv()
        exchange(g, k, 3).start()
        meanwhile()
        total = diagonal * oper[g] + mm(buf[g, k, 0], mats[0])
        exchange(g, k, 1).wait_recv()
        total += mm(buf[g, k, 1], mats[1])
        total += mm(buf[g, k, 2], mats[2])
        exchange(g, k, 3).wait_recv()
        total += mm(buf[g, k, 3], mats[3])
        for role in (1, 2, 3):
            exchange(g, k, role).wait_send()
        return total

    def wave_copy(t, d):
        return pltpu.make_async_remote_copy(
            src_ref=wall.at[t, me_s],
            dst_ref=wall.at[t, me_s],
            send_sem=w_send.at[t, d],
            recv_sem=w_recv.at[t, me_s],
            device_id={"sub": lax.rem(me_s + d, ns)},
            device_id_type=MESH,
        )

    def send_waves(t):
        @pl.loop(1, ns)
        def _(d):
            wave_copy(t, d).start()

    def wait_waves(t):
        @pl.loop(1, ns)
        def _(d):
            origin = lax.rem(me_s + d, ns)
            pltpu.make_async_remote_copy(
                src_ref=wall.at[t, origin],
                dst_ref=wall.at[t, origin],
                send_sem=w_send.at[t, d],
                recv_sem=w_recv.at[t, origin],
                device_id={"sub": origin},
                device_id_type=MESH,
            ).wait_recv()

    def block_copy(ref, t, r, owner):
        return pltpu.make_async_remote_copy(
            src_ref=ref.at[owner],
            dst_ref=ref.at[owner],
            send_sem=i_send.at[t, r],
            recv_sem=i_recv.at[t, owner],
            device_id={"blk": roles[r]},
            device_id_type=MESH,
        )

    def share(ref, t):
        for r in (2, 3, 1):
            block_copy(ref, t, r, me).start()

    def wait_share(ref, t):
        for r in (1, 2, 3):
            block_copy(ref, t, r, roles[r]).wait_recv()

    square = (
        lax.broadcasted_iota(jnp.int32, (ports, ports), 0)
        == lax.broadcasted_iota(jnp.int32, (ports, ports), 1)
    )

    def column(row):
        spread = jnp.broadcast_to(row, (ports, ports))
        return jnp.sum(jnp.where(square, spread, jnp.zeros_like(spread)), axis=1, keepdims=True)

    def select(t):
        owner = column(par[...].astype(F32))

        def place(i, found):
            return jnp.where(owner == i.astype(F32), pos[i].astype(F32), found)

        located = lax.fori_loop(0, ns, place, jnp.zeros((ports, 1), F32))

        def pick(q, chosen):
            return jnp.where(located == q.astype(F32), wall[t, q].astype(F32), chosen)

        chosen = lax.fori_loop(0, ns, pick, jnp.zeros(wall.shape[2:], F32))
        iall[t, me] = chosen.astype(BF16)

    def inputs(t):
        for b in range(nb):
            value = iall[t, b]
            for f in range(steps):
                inc8[f, b * ports : (b + 1) * ports, :] = value[:, f * rows : (f + 1) * rows]
        for j in range(steps):
            factor = jnp.where(j < count, spacing_f, 0.0)
            rb[j] = (inc8[fine(j)].astype(F32) * factor).astype(BF16)

    def respond():
        drive = rb[...].reshape(steps * all_ports, rows)
        value = mm(t_hi[...], drive) + mm(t_lo[...], drive)
        samp[...] = zp[...] + value.reshape(steps, ports, rows)

    diagonal = dia[...]
    pick_ports = (
        lax.broadcasted_iota(jnp.int32, (ports, width), 1)
        == stride * lax.broadcasted_iota(jnp.int32, (ports, width), 0)
    ).astype(F32).astype(BF16)

    call[me] = jnp.broadcast_to(column(cpl[...]), call.shape[1:])
    first = z[...] + spacing_f * src[fine(0)].astype(F32)
    oper[0] = first

    pl.semaphore_wait(barrier, ns - 1 + nb - 1)
    post(0, 0, first)
    share(call, 2)
    send_waves(0)
    t_hi[...] = jnp.zeros_like(t_hi)
    t_lo[...] = jnp.zeros_like(t_lo)
    for load in loads:
        load.wait()

    def keep(h, k):
        value = oper[1 + h]
        scale = call[...].reshape(all_ports, call.shape[2])[h * rows : (h + 1) * rows, :1]
        hi, lo = split(scale * value)
        hs[k, h * rows : (h + 1) * rows, :] = hi
        p_hi[k, :, h * rows : (h + 1) * rows] = mm_nt(pick_ports, hi).astype(BF16)
        p_lo[k, :, h * rows : (h + 1) * rows] = mm_nt(pick_ports, lo).astype(BF16)

    for h in range(halves):
        node = stride * (lax.broadcasted_iota(jnp.int32, (rows, width), 0) + h * rows)
        lane = lax.broadcasted_iota(jnp.int32, (rows, width), 1)
        total = diagonal * (lane + me * width == node).astype(F32)
        for r, b in enumerate(roles):
            total += mm((lane + b * width == node).astype(F32).astype(BF16), mats[r])
        oper[1 + h] = total
        post(1 + h, 1, total)
    def sample(k):
        hi, lo = split(z[...])
        zp[k] = mm_nt(pick_ports, hi) + mm_nt(pick_ports, lo)

    def keep_last(k):
        @pl.when(k >= 0)
        def _():
            keep(halves - 1, k)

    wait_share(call, 2)
    for h in range(halves - 1):
        keep(h, 0)

    @pl.loop(0, steps)
    def _(i):
        total = jnp.where(i < count, finish(0, i, lambda: keep_last(i - 1)), z[...])
        z[...] = total

        @pl.when(i < steps - 1)
        def _():
            operand = total + spacing_f * src[fine(i + 1)].astype(F32)
            oper[0] = operand
            post(0, i + 1, operand)

        @pl.when(i == 0)
        def _():
            sample(0)

        @pl.when(i >= 1)
        def _():
            for h in range(halves):
                work = functools.partial(keep, h - 1, i) if h else functools.partial(sample, i)
                value = finish(1 + h, i, work)
                oper[1 + h] = value

                @pl.when(i < steps - 1)
                def _():
                    post(1 + h, i + 1, value)

        @pl.when(i == steps // 2 - 1)
        def _():
            wait_waves(0)
            select(0)
            share(iall.at[0], 0)

        @pl.when(i == steps // 2 + 1)
        def _():
            wait_share(iall.at[0], 0)
            inputs(0)

    keep(halves - 1, steps - 1)
    for k in range(steps):
        for j in range(k + 1):
            there = (
                slice(k * ports, (k + 1) * ports),
                slice(j * all_ports, (j + 1) * all_ports),
            )
            t_hi[there] = p_hi[k - j]
            t_lo[there] = p_lo[k - j]
    respond()
    for g in range(steps):
        wall[1, me_s, :, g * rows : (g + 1) * rows] = samp[held(g)].astype(BF16)
    send_waves(1)
    wait_waves(1)
    select(1)
    share(iall.at[1], 1)
    wait_share(iall.at[1], 1)
    inputs(1)
    respond()
    for g in range(steps):
        wav[0, :, g * rows : (g + 1) * rows] = samp[held(g)]
    unit = (
        lax.broadcasted_iota(jnp.int32, (rows, rows), 0)
        == lax.broadcasted_iota(jnp.int32, (rows, rows), 1)
    ).astype(F32).astype(BF16)
    for m in range(1, steps + 1):
        turned = mm_nt(unit, rb[jnp.maximum(count - m, 0)])
        lhs[:, (m - 1) * all_ports : m * all_ports] = jnp.where(m <= count, turned, 0.0).astype(BF16)
    last[0] = z[...] + mm(lhs[...], hs[...].reshape(steps * all_ports, width))

    for t in range(2):

        @pl.loop(1, ns)
        def _(d):
            wave_copy(t, d).wait_send()

        for r in (1, 2, 3):
            block_copy(iall.at[t], t, r, me).wait_send()
    for r in (1, 2, 3):
        block_copy(call, 2, r, me).wait_send()


def shards(ns, nb, initial_state, source, inverse_diag, inverse_off, coupling, initial_waves,
           bucket, partner, position_of):
    _, steps, rows, width = source.shape
    ports = coupling.shape[1]
    all_ports = ports * nb
    groups = 1 + all_ports // rows
    vmem = pl.BlockSpec(memory_space=pltpu.VMEM)
    dma = pltpu.SemaphoreType.DMA
    return pl.pallas_call(
        functools.partial(kernel, ns, nb),
        out_shape=(
            jax.ShapeDtypeStruct(initial_state.shape, F32),
            jax.ShapeDtypeStruct(initial_waves.shape, F32),
        ),
        in_specs=[pl.BlockSpec(memory_space=pltpu.HBM)] * 9,
        out_specs=(vmem, vmem),
        scratch_shapes=[
            pltpu.VMEM(source.shape[1:], BF16),
            pltpu.VMEM(inverse_diag.shape, F32),
            pltpu.VMEM(coupling.shape, F32),
            pltpu.VMEM(partner.shape, jnp.int32),
            pltpu.SMEM(bucket.shape, jnp.int32),
            pltpu.SMEM(position_of.shape, jnp.int32),
            pltpu.VMEM((nb, width, width), BF16),
            pltpu.VMEM((groups, steps, nb, rows, width), BF16),
            pltpu.VMEM((groups, rows, width), F32),
            pltpu.VMEM((rows, width), F32),
            pltpu.VMEM((steps, all_ports, width), BF16),
            pltpu.VMEM((steps, ports, all_ports), BF16),
            pltpu.VMEM((steps, ports, all_ports), BF16),
            pltpu.VMEM((steps * ports, steps * all_ports), BF16),
            pltpu.VMEM((steps * ports, steps * all_ports), BF16),
            pltpu.VMEM((steps, ports, rows), F32),
            pltpu.VMEM((steps, all_ports, rows), BF16),
            pltpu.VMEM((steps, all_ports, rows), BF16),
            pltpu.VMEM((steps, ports, rows), F32),
            pltpu.VMEM((2, ns) + initial_waves.shape[1:], BF16),
            pltpu.VMEM((2, nb) + initial_waves.shape[1:], BF16),
            pltpu.VMEM((nb, ports, 128), F32),
            pltpu.VMEM((rows, steps * all_ports), BF16),
            dma((8,)),
            dma((nb,)),
            dma((groups, 2, 3)),
            dma((groups, 2, 3)),
            dma((2, ns)),
            dma((2, ns)),
            dma((3, nb)),
            dma((3, nb)),
        ],
        compiler_params=pltpu.CompilerParams(
            collective_id=0, has_side_effects=True, vmem_limit_bytes=48 * 1024 * 1024
        ),
    )(initial_state, source, inverse_diag, inverse_off, coupling, initial_waves, bucket, partner,
      position_of)


def solution(mesh):
    return jax.shard_map(
        functools.partial(shards, mesh.shape["sub"], mesh.shape["blk"]),
        mesh=mesh,
        in_specs=(
            P("sub", None, "blk"),
            P("sub", None, None, "blk"),
            P("sub", "blk"),
            P("sub", None, "blk"),
            P("sub", "blk"),
            P("sub", "blk", None),
            P("sub"),
            P("sub", "blk"),
            P(),
        ),
        out_specs=(P("sub", None, "blk"), P("sub", "blk", None)),
        check_vma=False,
    )
```

```python
import functools

import jax
import jax.numpy as jnp
from jax import lax
from jax.experimental import pallas as pl
from jax.experimental.pallas import tpu as pltpu
from jax.sharding import PartitionSpec as P

MESH = pl.DeviceIdType.MESH
BF16 = jnp.bfloat16
F32 = jnp.float32


def mm(a, b):
    return jnp.dot(a, b, preferred_element_type=F32)


def mm_nt(a, b):
    return lax.dot_general(a, b, (((1,), (1,)), ((), ())), preferred_element_type=F32)


def split(v):
    hi = v.astype(BF16)
    return hi, (v - hi.astype(F32)).astype(BF16)


def kernel(
    ns, nb,
    x0_in, src_in, dia_in, moff, cpl_in, w0_in, bkt_in, par_in, pos_in,
    last, wav,
    src, dia, cpl, par, bkt, pos, mats, buf, oper, z, hs, p_hi, p_lo, t_hi, t_lo, zp, inc8, rb, samp, wall, iall, call, lhs,
    a_sem, m_sem, x_send, x_recv, w_send, w_recv, i_send, i_recv,
):
    me_s, me = lax.axis_index("sub"), lax.axis_index("blk")
    steps, rows, width = src.shape
    ports = cpl.shape[1]
    stride = width // ports
    all_ports = ports * nb
    halves = all_ports // rows
    near = me + 1 - 2 * lax.rem(me, 2)
    across = lax.rem(me + 2, nb)
    roles = (me, near, across, nb - 1 - me)

    args = [
        pltpu.make_async_copy(there, here, a_sem.at[r])
        for r, (there, here) in enumerate(
            (
                (bkt_in, bkt),
                (x0_in.at[0], z),
                (src_in.at[0], src),
                (cpl_in, cpl),
                (w0_in.at[0], wall.at[0, me_s]),
                (dia_in, dia),
                (par_in, par),
                (pos_in, pos),
            )
        )
    ]
    for load in args:
        load.start()
    loads = [
        pltpu.make_async_copy(
            moff.at[0, pl.ds(pl.multiple_of(b * width, width), width)], mats.at[r], m_sem.at[r]
        )
        for r, b in enumerate(roles)
    ]
    for load in loads:
        load.start()

    barrier = pltpu.get_barrier_semaphore()

    @pl.loop(1, ns)
    def _(d):
        pl.semaphore_signal(
            barrier, inc=1, device_id={"sub": lax.rem(me_s + d, ns)}, device_id_type=MESH
        )

    for peer in roles[1:]:
        pl.semaphore_signal(barrier, inc=1, device_id={"blk": peer}, device_id_type=MESH)

    for load in args:
        load.wait()
    bucket = bkt[0]
    count = jnp.where(bucket == 0, steps // 4, jnp.where(bucket == 1, steps // 2, steps))
    spacing = jnp.where(bucket == 0, 4, jnp.where(bucket == 1, 2, 1))
    spacing_f = spacing.astype(F32)

    def fine(j):
        return jnp.minimum((j + 1) * spacing - 1, steps - 1)

    def held(g):
        return jnp.where(bucket == 0, g // 4, jnp.where(bucket == 1, g // 2, g))

    def exchange(g, k, role):
        start, end, peer = {1: (0, 1, near), 2: (0, 2, across), 3: (2, 3, near)}[role]
        parity = lax.rem(k, 2)
        return pltpu.make_async_remote_copy(
            src_ref=buf.at[g, k, start],
            dst_ref=buf.at[g, k, end],
            send_sem=x_send.at[g, parity, role - 1],
            recv_sem=x_recv.at[g, parity, role - 1],
            device_id={"blk": peer},
            device_id_type=MESH,
        )

    def post(g, k, value):
        buf[g, k, 0] = value.astype(BF16)
        exchange(g, k, 2).start()
        exchange(g, k, 1).start()

    def finish(g, k, meanwhile):
        exchange(g, k, 2).wait_recv()
        exchange(g, k, 3).start()
        meanwhile()
        total = diagonal * oper[g] + mm(buf[g, k, 0], mats[0])
        exchange(g, k, 1).wait_recv()
        total += mm(buf[g, k, 1], mats[1])
        total += mm(buf[g, k, 2], mats[2])
        exchange(g, k, 3).wait_recv()
        total += mm(buf[g, k, 3], mats[3])
        for role in (1, 2, 3):
            exchange(g, k, role).wait_send()
        return total

    def wave_copy(t, d):
        return pltpu.make_async_remote_copy(
            src_ref=wall.at[t, me_s],
            dst_ref=wall.at[t, me_s],
            send_sem=w_send.at[t, d],
            recv_sem=w_recv.at[t, me_s],
            device_id={"sub": lax.rem(me_s + d, ns)},
            device_id_type=MESH,
        )

    def send_waves(t):
        @pl.loop(1, ns)
        def _(d):
            wave_copy(t, d).start()

    def wait_waves(t):
        @pl.loop(1, ns)
        def _(d):
            origin = lax.rem(me_s + d, ns)
            pltpu.make_async_remote_copy(
                src_ref=wall.at[t, origin],
                dst_ref=wall.at[t, origin],
                send_sem=w_send.at[t, d],
                recv_sem=w_recv.at[t, origin],
                device_id={"sub": origin},
                device_id_type=MESH,
            ).wait_recv()

    def block_copy(ref, t, r, owner):
        return pltpu.make_async_remote_copy(
            src_ref=ref.at[owner],
            dst_ref=ref.at[owner],
            send_sem=i_send.at[t, r],
            recv_sem=i_recv.at[t, owner],
            device_id={"blk": roles[r]},
            device_id_type=MESH,
        )

    def share(ref, t):
        for r in (2, 3, 1):
            block_copy(ref, t, r, me).start()

    def wait_share(ref, t):
        for r in (1, 2, 3):
            block_copy(ref, t, r, roles[r]).wait_recv()

    square = (
        lax.broadcasted_iota(jnp.int32, (ports, ports), 0)
        == lax.broadcasted_iota(jnp.int32, (ports, ports), 1)
    )

    def column(row):
        spread = jnp.broadcast_to(row, (ports, ports))
        return jnp.sum(jnp.where(square, spread, jnp.zeros_like(spread)), axis=1, keepdims=True)

    def select(t):
        owner = column(par[...].astype(F32))

        def place(i, found):
            return jnp.where(owner == i.astype(F32), pos[i].astype(F32), found)

        located = lax.fori_loop(0, ns, place, jnp.zeros((ports, 1), F32))

        def pick(q, chosen):
            return jnp.where(located == q.astype(F32), wall[t, q].astype(F32), chosen)

        chosen = lax.fori_loop(0, ns, pick, jnp.zeros(wall.shape[2:], F32))
        iall[t, me] = chosen.astype(BF16)

    def inputs(t):
        for b in range(nb):
            value = iall[t, b]
            for f in range(steps):
                inc8[f, b * ports : (b + 1) * ports, :] = value[:, f * rows : (f + 1) * rows]
        for j in range(steps):
            factor = jnp.where(j < count, spacing_f, 0.0)
            rb[j] = (inc8[fine(j)].astype(F32) * factor).astype(BF16)

    def respond():
        drive = rb[...].reshape(steps * all_ports, rows)
        value = mm(t_hi[...], drive) + mm(t_lo[...], drive)
        samp[...] = zp[...] + value.reshape(steps, ports, rows)

    diagonal = dia[...]
    pick_ports = (
        lax.broadcasted_iota(jnp.int32, (ports, width), 1)
        == stride * lax.broadcasted_iota(jnp.int32, (ports, width), 0)
    ).astype(F32).astype(BF16)

    call[me] = jnp.broadcast_to(column(cpl[...]), call.shape[1:])
    first = z[...] + spacing_f * src[fine(0)].astype(F32)
    oper[0] = first

    pl.semaphore_wait(barrier, ns - 1 + nb - 1)
    post(0, 0, first)
    share(call, 2)
    send_waves(0)
    t_hi[...] = jnp.zeros_like(t_hi)
    t_lo[...] = jnp.zeros_like(t_lo)
    for load in loads:
        load.wait()

    def keep(h, k):
        value = oper[1 + h]
        scale = call[...].reshape(all_ports, call.shape[2])[h * rows : (h + 1) * rows, :1]
        hi, lo = split(scale * value)
        hs[k, h * rows : (h + 1) * rows, :] = hi
        p_hi[k, :, h * rows : (h + 1) * rows] = mm_nt(pick_ports, hi).astype(BF16)
        p_lo[k, :, h * rows : (h + 1) * rows] = mm_nt(pick_ports, lo).astype(BF16)

    for h in range(halves):
        node = stride * (lax.broadcasted_iota(jnp.int32, (rows, width), 0) + h * rows)
        lane = lax.broadcasted_iota(jnp.int32, (rows, width), 1)
        total = diagonal * (lane + me * width == node).astype(F32)
        for r, b in enumerate(roles):
            total += mm((lane + b * width == node).astype(F32).astype(BF16), mats[r])
        oper[1 + h] = total
        post(1 + h, 1, total)
    def sample(k):
        hi, lo = split(z[...])
        zp[k] = mm_nt(pick_ports, hi) + mm_nt(pick_ports, lo)

    def keep_last(k):
        @pl.when(k >= 0)
        def _():
            keep(halves - 1, k)

    wait_share(call, 2)
    for h in range(halves - 1):
        keep(h, 0)

    @pl.loop(0, steps)
    def _(i):
        total = jnp.where(i < count, finish(0, i, lambda: keep_last(i - 1)), z[...])
        z[...] = total

        @pl.when(i < steps - 1)
        def _():
            operand = total + spacing_f * src[fine(i + 1)].astype(F32)
            oper[0] = operand
            post(0, i + 1, operand)

        @pl.when(i == 0)
        def _():
            sample(0)

        @pl.when(i >= 1)
        def _():
            for h in range(halves):
                work = functools.partial(keep, h - 1, i) if h else functools.partial(sample, i)
                value = finish(1 + h, i, work)
                oper[1 + h] = value

                @pl.when(i < steps - 1)
                def _():
                    post(1 + h, i + 1, value)

        @pl.when(i == steps // 2 - 1)
        def _():
            wait_waves(0)
            select(0)
            share(iall.at[0], 0)

        @pl.when(i == steps // 2 + 1)
        def _():
            wait_share(iall.at[0], 0)
            inputs(0)

    keep(halves - 1, steps - 1)
    for k in range(steps):
        for j in range(k + 1):
            there = (
                slice(k * ports, (k + 1) * ports),
                slice(j * all_ports, (j + 1) * all_ports),
            )
            t_hi[there] = p_hi[k - j]
            t_lo[there] = p_lo[k - j]
    respond()
    for g in range(steps):
        wall[1, me_s, :, g * rows : (g + 1) * rows] = samp[held(g)].astype(BF16)
    send_waves(1)
    wait_waves(1)
    select(1)
    share(iall.at[1], 1)
    wait_share(iall.at[1], 1)
    inputs(1)
    respond()
    for g in range(steps):
        wav[0, :, g * rows : (g + 1) * rows] = samp[held(g)]
    unit = (
        lax.broadcasted_iota(jnp.int32, (rows, rows), 0)
        == lax.broadcasted_iota(jnp.int32, (rows, rows), 1)
    ).astype(F32).astype(BF16)
    for m in range(1, steps + 1):
        turned = mm_nt(unit, rb[jnp.maximum(count - m, 0)])
        lhs[:, (m - 1) * all_ports : m * all_ports] = jnp.where(m <= count, turned, 0.0).astype(BF16)
    last[0] = z[...] + mm(lhs[...], hs[...].reshape(steps * all_ports, width))

    for t in range(2):

        @pl.loop(1, ns)
        def _(d):
            wave_copy(t, d).wait_send()

        for r in (1, 2, 3):
            block_copy(iall.at[t], t, r, me).wait_send()
    for r in (1, 2, 3):
        block_copy(call, 2, r, me).wait_send()


def shards(ns, nb, initial_state, source, inverse_diag, inverse_off, coupling, initial_waves,
           bucket, partner, position_of):
    _, steps, rows, width = source.shape
    ports = coupling.shape[1]
    all_ports = ports * nb
    groups = 1 + all_ports // rows
    vmem = pl.BlockSpec(memory_space=pltpu.VMEM)
    dma = pltpu.SemaphoreType.DMA
    return pl.pallas_call(
        functools.partial(kernel, ns, nb),
        out_shape=(
            jax.ShapeDtypeStruct(initial_state.shape, F32),
            jax.ShapeDtypeStruct(initial_waves.shape, F32),
        ),
        in_specs=[pl.BlockSpec(memory_space=pltpu.HBM)] * 9,
        out_specs=(vmem, vmem),
        scratch_shapes=[
            pltpu.VMEM(source.shape[1:], BF16),
            pltpu.VMEM(inverse_diag.shape, F32),
            pltpu.VMEM(coupling.shape, F32),
            pltpu.VMEM(partner.shape, jnp.int32),
            pltpu.SMEM(bucket.shape, jnp.int32),
            pltpu.SMEM(position_of.shape, jnp.int32),
            pltpu.VMEM((nb, width, width), BF16),
            pltpu.VMEM((groups, steps, nb, rows, width), BF16),
            pltpu.VMEM((groups, rows, width), F32),
            pltpu.VMEM((rows, width), F32),
            pltpu.VMEM((steps, all_ports, width), BF16),
            pltpu.VMEM((steps, ports, all_ports), BF16),
            pltpu.VMEM((steps, ports, all_ports), BF16),
            pltpu.VMEM((steps * ports, steps * all_ports), BF16),
            pltpu.VMEM((steps * ports, steps * all_ports), BF16),
            pltpu.VMEM((steps, ports, rows), F32),
            pltpu.VMEM((steps, all_ports, rows), BF16),
            pltpu.VMEM((steps, all_ports, rows), BF16),
            pltpu.VMEM((steps, ports, rows), F32),
            pltpu.VMEM((2, ns) + initial_waves.shape[1:], BF16),
            pltpu.VMEM((2, nb) + initial_waves.shape[1:], BF16),
            pltpu.VMEM((nb, ports, 128), F32),
            pltpu.VMEM((rows, steps * all_ports), BF16),
            dma((8,)),
            dma((nb,)),
            dma((groups, 2, 3)),
            dma((groups, 2, 3)),
            dma((2, ns)),
            dma((2, ns)),
            dma((3, nb)),
            dma((3, nb)),
        ],
        compiler_params=pltpu.CompilerParams(
            collective_id=0, has_side_effects=True, vmem_limit_bytes=67043328
        ),
    )(initial_state, source, inverse_diag, inverse_off, coupling, initial_waves, bucket, partner,
      position_of)


def solution(mesh):
    return jax.shard_map(
        functools.partial(shards, mesh.shape["sub"], mesh.shape["blk"]),
        mesh=mesh,
        in_specs=(
            P("sub", None, "blk"),
            P("sub", None, None, "blk"),
            P("sub", "blk"),
            P("sub", None, "blk"),
            P("sub", "blk"),
            P("sub", "blk", None),
            P("sub"),
            P("sub", "blk"),
            P(),
        ),
        out_specs=(P("sub", None, "blk"), P("sub", "blk", None)),
        check_vma=False,
    )
```

```python
import functools

import jax
import jax.numpy as jnp
from jax import lax
from jax.experimental import pallas as pl
from jax.experimental.pallas import tpu as pltpu
from jax.sharding import PartitionSpec as P

MESH = pl.DeviceIdType.MESH
BF16 = jnp.bfloat16
F32 = jnp.float32


def mm(a, b):
    return jnp.dot(a, b, preferred_element_type=F32)


def mm_nt(a, b):
    return lax.dot_general(a, b, (((1,), (1,)), ((), ())), preferred_element_type=F32)


def split(v):
    hi = v.astype(BF16)
    return hi, (v - hi.astype(F32)).astype(BF16)


def kernel(
    ns, nb,
    x0_in, src_in, dia_in, moff, cpl_in, w0_in, bkt_in, par_in, pos_in,
    last, wav,
    src, dia, cpl, par, bkt, pos, mats, buf, oper, z, hs, p_hi, p_lo, t_hi, t_lo, zp, inc8, rb, samp, wall, iall, call, lhs,
    a_sem, m_sem, x_send, x_recv, w_send, w_recv, i_send, i_recv,
):
    me_s, me = lax.axis_index("sub"), lax.axis_index("blk")
    steps, rows, width = src.shape
    ports = cpl.shape[1]
    stride = width // ports
    all_ports = ports * nb
    halves = all_ports // rows
    near = me + 1 - 2 * lax.rem(me, 2)
    across = lax.rem(me + 2, nb)
    roles = (me, near, across, nb - 1 - me)

    args = [
        pltpu.make_async_copy(there, here, a_sem.at[r])
        for r, (there, here) in enumerate(
            (
                (bkt_in, bkt),
                (x0_in.at[0], z),
                (src_in.at[0], src),
                (cpl_in, cpl),
                (w0_in.at[0], wall.at[0, me_s]),
                (dia_in, dia),
                (par_in, par),
                (pos_in, pos),
            )
        )
    ]
    for load in args:
        load.start()
    loads = [
        pltpu.make_async_copy(
            moff.at[0, pl.ds(pl.multiple_of(b * width, width), width)], mats.at[r], m_sem.at[r]
        )
        for r, b in enumerate(roles)
    ]
    for load in loads:
        load.start()

    barrier = pltpu.get_barrier_semaphore()

    @pl.loop(1, ns)
    def _(d):
        pl.semaphore_signal(
            barrier, inc=1, device_id={"sub": lax.rem(me_s + d, ns)}, device_id_type=MESH
        )

    for peer in roles[1:]:
        pl.semaphore_signal(barrier, inc=1, device_id={"blk": peer}, device_id_type=MESH)

    for load in args:
        load.wait()
    bucket = bkt[0]
    count = jnp.where(bucket == 0, steps // 4, jnp.where(bucket == 1, steps // 2, steps))
    spacing = jnp.where(bucket == 0, 4, jnp.where(bucket == 1, 2, 1))
    spacing_f = spacing.astype(F32)

    def fine(j):
        return jnp.minimum((j + 1) * spacing - 1, steps - 1)

    def held(g):
        return jnp.where(bucket == 0, g // 4, jnp.where(bucket == 1, g // 2, g))

    def exchange(g, k, role):
        start, end, peer = {1: (0, 1, near), 2: (0, 2, across), 3: (2, 3, near)}[role]
        parity = lax.rem(k, 2)
        return pltpu.make_async_remote_copy(
            src_ref=buf.at[g, k, start],
            dst_ref=buf.at[g, k, end],
            send_sem=x_send.at[g, parity, role - 1],
            recv_sem=x_recv.at[g, parity, role - 1],
            device_id={"blk": peer},
            device_id_type=MESH,
        )

    def post(g, k, value):
        buf[g, k, 0] = value.astype(BF16)
        exchange(g, k, 2).start()
        exchange(g, k, 1).start()

    def finish(g, k, meanwhile):
        exchange(g, k, 2).wait_recv()
        exchange(g, k, 3).start()
        meanwhile()
        total = diagonal * oper[g] + mm(buf[g, k, 0], mats[0])
        exchange(g, k, 1).wait_recv()
        total += mm(buf[g, k, 1], mats[1])
        total += mm(buf[g, k, 2], mats[2])
        exchange(g, k, 3).wait_recv()
        total += mm(buf[g, k, 3], mats[3])
        for role in (1, 2, 3):
            exchange(g, k, role).wait_send()
        return total

    cut = (steps - 2) * rows
    lanes = (slice(0, steps * rows), slice(0, cut), slice(cut, steps * rows))

    def wave_part(t, owner):
        return wall.at[min(t, 1), owner, :, lanes[t]]

    def block_part(t, owner):
        return call.at[owner] if t == 3 else iall.at[min(t, 1), owner, :, lanes[t]]

    def wave_copy(t, d, owner, peer):
        return pltpu.make_async_remote_copy(
            src_ref=wave_part(t, owner),
            dst_ref=wave_part(t, owner),
            send_sem=w_send.at[t, d],
            recv_sem=w_recv.at[t, owner],
            device_id={"sub": peer},
            device_id_type=MESH,
        )

    def send_waves(t):
        @pl.loop(1, ns)
        def _(d):
            wave_copy(t, d, me_s, lax.rem(me_s + d, ns)).start()

    def wait_waves(t):
        @pl.loop(1, ns)
        def _(d):
            origin = lax.rem(me_s + d, ns)
            wave_copy(t, d, origin, origin).wait_recv()

    def block_copy(t, r, owner):
        return pltpu.make_async_remote_copy(
            src_ref=block_part(t, owner),
            dst_ref=block_part(t, owner),
            send_sem=i_send.at[t, r],
            recv_sem=i_recv.at[t, owner],
            device_id={"blk": roles[r]},
            device_id_type=MESH,
        )

    def share(t):
        for r in (2, 3, 1):
            block_copy(t, r, me).start()

    def wait_share(t):
        for r in (1, 2, 3):
            block_copy(t, r, roles[r]).wait_recv()

    square = (
        lax.broadcasted_iota(jnp.int32, (ports, ports), 0)
        == lax.broadcasted_iota(jnp.int32, (ports, ports), 1)
    )

    def column(row):
        spread = jnp.broadcast_to(row, (ports, ports))
        return jnp.sum(jnp.where(square, spread, jnp.zeros_like(spread)), axis=1, keepdims=True)

    def select(t):
        owner = column(par[...].astype(F32))

        def place(i, found):
            return jnp.where(owner == i.astype(F32), pos[i].astype(F32), found)

        located = lax.fori_loop(0, ns, place, jnp.zeros((ports, 1), F32))

        def pick(q, chosen):
            return jnp.where(located == q.astype(F32), wall[min(t, 1), q, :, lanes[t]].astype(F32), chosen)

        chosen = lax.fori_loop(0, ns, pick, jnp.zeros((ports, lanes[t].stop - lanes[t].start), F32))
        iall[min(t, 1), me, :, lanes[t]] = chosen.astype(BF16)

    def inputs(t):
        for b in range(nb):
            value = iall[t, b]
            for f in range(steps):
                inc8[f, b * ports : (b + 1) * ports, :] = value[:, f * rows : (f + 1) * rows]
        for j in range(steps):
            factor = jnp.where(j < count, spacing_f, 0.0)
            rb[j] = (inc8[fine(j)].astype(F32) * factor).astype(BF16)

    def toeplitz(low, high):
        for k in range(low, high):
            for j in range(k + 1):
                there = (
                    slice(k * ports, (k + 1) * ports),
                    slice(j * all_ports, (j + 1) * all_ports),
                )
                t_hi[there] = p_hi[k - j]
                t_lo[there] = p_lo[k - j]

    def respond(low, high):
        drive = rb[:high].reshape(high * all_ports, rows)
        there = (slice(low * ports, high * ports), slice(0, high * all_ports))
        value = mm(t_hi[there], drive) + mm(t_lo[there], drive)
        samp[low:high] = zp[low:high] + value.reshape(high - low, ports, rows)

    def waves_out(low, high):
        for g in range(low, high):
            wall[1, me_s, :, g * rows : (g + 1) * rows] = samp[held(g)].astype(BF16)

    diagonal = dia[...]
    pick_ports = (
        lax.broadcasted_iota(jnp.int32, (ports, width), 1)
        == stride * lax.broadcasted_iota(jnp.int32, (ports, width), 0)
    ).astype(F32).astype(BF16)

    call[me] = jnp.broadcast_to(column(cpl[...]), call.shape[1:])
    first = z[...] + spacing_f * src[fine(0)].astype(F32)
    oper[0] = first

    pl.semaphore_wait(barrier, ns - 1 + nb - 1)
    post(0, 0, first)
    share(3)
    send_waves(0)
    t_hi[...] = jnp.zeros_like(t_hi)
    t_lo[...] = jnp.zeros_like(t_lo)
    for load in loads:
        load.wait()

    def keep(h, k):
        value = oper[1 + h]
        scale = call[...].reshape(all_ports, call.shape[2])[h * rows : (h + 1) * rows, :1]
        hi, lo = split(scale * value)
        hs[k, h * rows : (h + 1) * rows, :] = hi
        p_hi[k, :, h * rows : (h + 1) * rows] = mm_nt(pick_ports, hi).astype(BF16)
        p_lo[k, :, h * rows : (h + 1) * rows] = mm_nt(pick_ports, lo).astype(BF16)

    for h in range(halves):
        node = stride * (lax.broadcasted_iota(jnp.int32, (rows, width), 0) + h * rows)
        lane = lax.broadcasted_iota(jnp.int32, (rows, width), 1)
        total = diagonal * (lane + me * width == node).astype(F32)
        for r, b in enumerate(roles):
            total += mm((lane + b * width == node).astype(F32).astype(BF16), mats[r])
        oper[1 + h] = total
        post(1 + h, 1, total)
    def sample(k):
        hi, lo = split(z[...])
        zp[k] = mm_nt(pick_ports, hi) + mm_nt(pick_ports, lo)

    def keep_last(k):
        @pl.when(k >= 0)
        def _():
            keep(halves - 1, k)

    wait_share(3)
    for h in range(halves - 1):
        keep(h, 0)

    @pl.loop(0, steps)
    def _(i):
        total = jnp.where(i < count, finish(0, i, lambda: keep_last(i - 1)), z[...])
        z[...] = total

        @pl.when(i < steps - 1)
        def _():
            operand = total + spacing_f * src[fine(i + 1)].astype(F32)
            oper[0] = operand
            post(0, i + 1, operand)

        @pl.when(i == 0)
        def _():
            sample(0)

        @pl.when(i >= 1)
        def _():
            for h in range(halves):
                work = functools.partial(keep, h - 1, i) if h else functools.partial(sample, i)
                value = finish(1 + h, i, work)
                oper[1 + h] = value

                @pl.when(i < steps - 1)
                def _():
                    post(1 + h, i + 1, value)

        @pl.when(i == steps // 2 - 1)
        def _():
            wait_waves(0)
            select(0)
            share(0)

        @pl.when(i == steps // 2 + 1)
        def _():
            wait_share(0)
            inputs(0)

        @pl.when(i == steps - 2)
        def _():
            toeplitz(0, steps - 2)
            respond(0, steps - 2)
            waves_out(0, steps - 2)
            send_waves(1)

    keep(halves - 1, steps - 1)
    toeplitz(steps - 2, steps)
    respond(steps - 2, steps)
    waves_out(steps - 2, steps)
    send_waves(2)
    wait_waves(1)
    select(1)
    share(1)
    wait_waves(2)
    select(2)
    share(2)
    wait_share(1)
    wait_share(2)
    inputs(1)
    respond(0, steps)
    for g in range(steps):
        wav[0, :, g * rows : (g + 1) * rows] = samp[held(g)]
    unit = (
        lax.broadcasted_iota(jnp.int32, (rows, rows), 0)
        == lax.broadcasted_iota(jnp.int32, (rows, rows), 1)
    ).astype(F32).astype(BF16)
    for m in range(1, steps + 1):
        turned = mm_nt(unit, rb[jnp.maximum(count - m, 0)])
        lhs[:, (m - 1) * all_ports : m * all_ports] = jnp.where(m <= count, turned, 0.0).astype(BF16)
    last[0] = z[...] + mm(lhs[...], hs[...].reshape(steps * all_ports, width))

    for t in range(3):

        @pl.loop(1, ns)
        def _(d):
            wave_copy(t, d, me_s, lax.rem(me_s + d, ns)).wait_send()

    for t in range(4):
        for r in (1, 2, 3):
            block_copy(t, r, me).wait_send()


def shards(ns, nb, initial_state, source, inverse_diag, inverse_off, coupling, initial_waves,
           bucket, partner, position_of):
    _, steps, rows, width = source.shape
    ports = coupling.shape[1]
    all_ports = ports * nb
    groups = 1 + all_ports // rows
    vmem = pl.BlockSpec(memory_space=pltpu.VMEM)
    dma = pltpu.SemaphoreType.DMA
    return pl.pallas_call(
        functools.partial(kernel, ns, nb),
        out_shape=(
            jax.ShapeDtypeStruct(initial_state.shape, F32),
            jax.ShapeDtypeStruct(initial_waves.shape, F32),
        ),
        in_specs=[pl.BlockSpec(memory_space=pltpu.HBM)] * 9,
        out_specs=(vmem, vmem),
        scratch_shapes=[
            pltpu.VMEM(source.shape[1:], BF16),
            pltpu.VMEM(inverse_diag.shape, F32),
            pltpu.VMEM(coupling.shape, F32),
            pltpu.VMEM(partner.shape, jnp.int32),
            pltpu.SMEM(bucket.shape, jnp.int32),
            pltpu.SMEM(position_of.shape, jnp.int32),
            pltpu.VMEM((nb, width, width), BF16),
            pltpu.VMEM((groups, steps, nb, rows, width), BF16),
            pltpu.VMEM((groups, rows, width), F32),
            pltpu.VMEM((rows, width), F32),
            pltpu.VMEM((steps, all_ports, width), BF16),
            pltpu.VMEM((steps, ports, all_ports), BF16),
            pltpu.VMEM((steps, ports, all_ports), BF16),
            pltpu.VMEM((steps * ports, steps * all_ports), BF16),
            pltpu.VMEM((steps * ports, steps * all_ports), BF16),
            pltpu.VMEM((steps, ports, rows), F32),
            pltpu.VMEM((steps, all_ports, rows), BF16),
            pltpu.VMEM((steps, all_ports, rows), BF16),
            pltpu.VMEM((steps, ports, rows), F32),
            pltpu.VMEM((2, ns) + initial_waves.shape[1:], BF16),
            pltpu.VMEM((2, nb) + initial_waves.shape[1:], BF16),
            pltpu.VMEM((nb, ports, 128), F32),
            pltpu.VMEM((rows, steps * all_ports), BF16),
            dma((8,)),
            dma((nb,)),
            dma((groups, 2, 3)),
            dma((groups, 2, 3)),
            dma((3, ns)),
            dma((3, ns)),
            dma((4, nb)),
            dma((4, nb)),
        ],
        compiler_params=pltpu.CompilerParams(
            collective_id=0, has_side_effects=True, vmem_limit_bytes=67043328
        ),
    )(initial_state, source, inverse_diag, inverse_off, coupling, initial_waves, bucket, partner,
      position_of)


def solution(mesh):
    return jax.shard_map(
        functools.partial(shards, mesh.shape["sub"], mesh.shape["blk"]),
        mesh=mesh,
        in_specs=(
            P("sub", None, "blk"),
            P("sub", None, None, "blk"),
            P("sub", "blk"),
            P("sub", None, "blk"),
            P("sub", "blk"),
            P("sub", "blk", None),
            P("sub"),
            P("sub", "blk"),
            P(),
        ),
        out_specs=(P("sub", None, "blk"), P("sub", "blk", None)),
        check_vma=False,
    )
```
